256 devices in a mesh: inst: 8 (over y, x_lo), scen: 32 (over x_hi, z, core).
Axes of the slice: x: 4 (x_hi: 2, x_lo: 2; x = x_hi * 2 + x_lo), y: 4, z: 8, core: 2. Of those that a mesh axis runs over, the one named last changes fastest.
Arguments:
- positions: int32 [512, 16384], P(None, 'inst'), may hold values from -50 to 50
- holding_block_grid: int32 [8, 128], P(None, 'inst'), may hold values 0 or 1
- risk: float32 [16384, 32768], P('inst', 'scen'), may hold values from -64 to 64
Outputs:
- margin: float32 [512], P('inst')
- gradient: float32 [512, 16384], P('scen', 'inst')
The draws below stay inside these ranges and needn't reach their ends.
All inputs are finite; a program needn't handle non-finite values. No bound on the sum of `holding_block_grid` on one device may be relied on, other than what follows from the above.
Results may differ from the reference program's by a relative error of at most 0.0003.
Values sent between devices are 32-bit elements; how exact they have to be, the bound alone decides.
No kernel may reach another device: no remote copies, remote signals or barrier semaphores. Data moves between devices by JAX's collectives and lax.ppermute only.
A program may use at most 64 MiB of HBM per device.

```python
import math
import jax
import jax.numpy as jnp
from jax import lax

ACC = 512
INSTRUMENT_TOTAL = 16384
ABLK = 64
IBLK = 128
SCEN = 32768


def draw_risk(key, part):
    first, second, third = jax.random.split(jax.random.fold_in(key, 17), 3)
    row_scale = jnp.exp(jax.random.uniform(second, (INSTRUMENT_TOTAL, 1), jnp.float32, jnp.log(0.3), jnp.log(3.0)))
    jitter = jnp.exp(jax.random.uniform(third, (1, SCEN), jnp.float32, jnp.log(0.9), jnp.log(1.1)))
    position = jnp.arange(SCEN, dtype=jnp.float32) / SCEN
    base = jnp.clip(jax.random.normal(first, (INSTRUMENT_TOTAL, SCEN), jnp.float32), -6.0, 6.0)
    ramp = jnp.sqrt(1.0 + 2.2 * position)
    result = 0.25 * base * row_scale * (jitter * ramp[None, :])
    return result


def with_ends(values, rng, low, high):
    dims = values.shape
    index_at = [jax.random.randint(jax.random.fold_in(rng, axis), (), 0, dims[axis]) for axis in range(len(dims))]
    values = values.at[tuple(index_at)].set(low)
    longest = dims.index(max(dims))
    index_at[longest] = (index_at[longest] + 1) % dims[longest]
    return values.at[tuple(index_at)].set(high)


def setup_inputs(seed: int = 0) -> dict:
    splits = jax.random.split(jax.random.key(seed), 4)
    return {
        "positions": with_ends(jax.random.randint(splits[0], (ACC, INSTRUMENT_TOTAL), -50, 51), jax.random.fold_in(splits[0], 1), -50, 50).astype(jnp.int32),
        "holding_block_grid": with_ends((jax.random.randint(splits[1], (ACC // ABLK, INSTRUMENT_TOTAL // IBLK), 0, 4) < 3).astype(jnp.int32), jax.random.fold_in(splits[1], 1), 0, 1),
        "risk": draw_risk(jax.random.fold_in(splits[3], 71), 0),
    }


def reference(positions, holding_block_grid, risk):
    live_mask = jnp.repeat(jnp.repeat(holding_block_grid, ABLK, axis=0), IBLK, axis=1)
    held = (positions * live_mask).astype(jnp.float32)
    profit_and_losses = jnp.dot(held, risk, precision=lax.Precision.HIGHEST, preferred_element_type=jnp.float32)
    softness_level = 8.0 * math.sqrt(INSTRUMENT_TOTAL)
    tail_logits = -profit_and_losses / softness_level
    peak = lax.optimization_barrier(jnp.max(tail_logits, axis=1))
    shifted = jnp.exp(tail_logits - peak[:, None])
    total = lax.optimization_barrier(jnp.sum(shifted, axis=1))
    margin = peak + jnp.log(total) - math.log(SCEN)
    weights = shifted / total[:, None]
    gradient = -jnp.einsum('as,is->ai', weights, risk, precision=lax.Precision.HIGHEST)
    return (margin, gradient)
```

```python
import functools
import math

import jax
import jax.numpy as jnp
from jax import lax
from jax.experimental import pallas as pl
from jax.experimental.pallas import tpu as pltpu
from jax.sharding import Mesh
from jax.sharding import PartitionSpec as P

Y, XL, XH, Z, C = 4, 2, 2, 8, 2
F32, BF16 = jnp.float32, jnp.bfloat16
VMEM = pl.BlockSpec(memory_space=pltpu.VMEM)
HBM = pl.BlockSpec(memory_space=pltpu.HBM)
SB = 256
EXT = 128


def send(x, axis, shift):
    n = lax.axis_size(axis)
    return lax.ppermute(x, axis, [(i, (i + shift) % n) for i in range(n)])


def halves(x):
    high = x.astype(BF16)
    return high, (x - high.astype(F32)).astype(BF16)


def pnl_kernel(
    pos, grid_in, risk, own, oth, b0, b1, b2, b3, posbuf, grid, rbuf, held, high, low, psem, gsem, rsem
):
    y, xl = lax.axis_index("y"), lax.axis_index("xl")
    steps = risk.shape[1] // SB

    def fetch(j, slot):
        return pltpu.make_async_copy(
            risk.at[:, pl.ds(pl.multiple_of(j * SB, SB), SB)], rbuf.at[slot], rsem.at[slot]
        )

    position_copy = pltpu.make_async_copy(pos, posbuf, psem)
    grid_copy = pltpu.make_async_copy(grid_in, grid, gsem)
    grid_copy.start()
    position_copy.start()
    fetch(0, 0).start()
    grid_copy.wait()
    position_copy.wait()
    at = 0
    blocks = [(0, d, e) for e in range(XL) for d in range(Y)]
    blocks += [(1, d, e) for d in range(Y) for e in range(XL)]
    for k, d, e in blocks:
        o = lax.rem(y + d, Y) * 2 + lax.rem(xl + e, XL)
        for pair in range(2):
            row = pl.multiple_of(o * 64 + pair * 32 + k * 8, 8)
            x = jnp.concatenate([posbuf[pl.ds(row, 8), :], posbuf[pl.ds(row + 16, 8), :]], axis=0)
            x = x.astype(F32)
            for i in range(pos.shape[1] // 128):
                live = grid[o, i].astype(F32)
                held[at : at + 16, i * 128 : (i + 1) * 128] = (
                    x[:, i * 128 : (i + 1) * 128] * live
                ).astype(BF16)
            at += 16

    @pl.loop(0, steps)
    def _(j):
        slot = lax.rem(j, 2)
        fetch(j, slot).wait()

        @pl.when(j + 1 < steps)
        def _():
            fetch(j + 1, 1 - slot).start()

        for i in range(0, risk.shape[0], 128):
            high[i : i + 128, :], low[i : i + 128, :] = halves(rbuf[slot, i : i + 128, :])
        cols = pl.ds(pl.multiple_of(j * SB, SB), SB)
        outs = ((0, own), (128, oth), (256, b0), (320, b1), (384, b2), (448, b3))
        acc = jnp.dot(held[...], high[...], preferred_element_type=F32)
        acc += jnp.dot(held[...], low[...], preferred_element_type=F32)
        for first, out in outs:
            out[:, cols] = acc[first : first + out.shape[0]]


def profits(positions, grid, risk):
    rows, n = risk.shape
    accounts = positions.shape[0]
    shape = lambda r: jax.ShapeDtypeStruct((r, n), F32)
    return pl.pallas_call(
        pnl_kernel,
        out_shape=[shape(128), shape(128)] + [shape(64)] * 4,
        in_specs=[HBM, HBM, HBM],
        out_specs=[VMEM] * 6,
        scratch_shapes=[
            pltpu.VMEM((accounts, rows), jnp.int32),
            pltpu.SMEM(grid.shape, jnp.int32),
            pltpu.VMEM((2, rows, SB), F32),
            pltpu.VMEM((accounts, rows), BF16),
            pltpu.VMEM((rows, SB), BF16),
            pltpu.VMEM((rows, SB), BF16),
            pltpu.SemaphoreType.DMA,
            pltpu.SemaphoreType.DMA,
            pltpu.SemaphoreType.DMA((2,)),
        ],
        compiler_params=pltpu.CompilerParams(vmem_limit_bytes=32 << 20),
        cost_estimate=pl.CostEstimate(
            flops=4 * accounts * rows * n, bytes_accessed=12 << 20, transcendentals=0
        ),
    )(*(pltpu.with_memory_space_constraint(a, pltpu.HBM) for a in (positions, grid, risk)))


def grad_kernel(softness, layout, *refs):
    pieces = refs[: len(layout)]
    risk, own, oth, rbuf, tails, stats, high, low, rsem = refs[len(layout) :]
    y, xl, xh, z, c = (lax.axis_index(a) for a in ("y", "xl", "xh", "z", "c"))
    n_inst, n_scen = risk.shape
    steps = n_inst // SB

    def fetch(j, slot):
        return pltpu.make_async_copy(
            risk.at[pl.ds(pl.multiple_of(j * SB, SB), SB), :], rbuf.at[slot], rsem.at[slot]
        )

    fetch(0, 0).start()
    half = XH * Z * 8
    lane = lax.broadcasted_iota(jnp.int32, (8, EXT), 1)
    owned = jnp.zeros((8, EXT), F32)
    for ref, blocks in zip(pieces, layout, strict=True):
        for b, (d, e) in enumerate(blocks):
            o = lax.rem(y + d, Y) * 2 + lax.rem(xl + e, XL)
            other_xh = jnp.where(o // 4 == xh, 0, 1)
            score = ref[b * 32 : b * 32 + 32, :] * (-1.0 / softness)
            peak = jnp.max(score, axis=1, keepdims=True)
            tail = jnp.exp(score - peak)
            total = jnp.sum(tail, axis=1, keepdims=True)
            for t in range(4):
                dz = lax.rem(lax.rem(o, 4) * 2 + t // 2 + Z - z, Z)
                dc = jnp.where(c == t % 2, 0, 1)
                row = pl.multiple_of(((dc * Z + dz) * XH + other_xh) * 8, 8)
                part = slice(t * 8, t * 8 + 8)
                tails[pl.ds(row, 8), :] = tail[part]
                stats[pl.ds(row, 8), :] = jnp.where(lane < 32, peak[part], jnp.where(lane < 64, total[part], 0.0))
                if (d, e) == (0, 0):
                    owned = jnp.where(lane == 64 + t, peak[part], owned)
                    owned = jnp.where(lane == 96 + t, total[part], owned)
    for out, first in ((own, 0), (oth, half)):
        out[:8, n_inst:] = jnp.where(lane < 64, stats[first : first + 8, :], owned)
        out[8:, n_inst:] = stats[first + 8 : first + half, :]
    for i in range(0, 2 * half, 64):
        high[i : i + 64, :], low[i : i + 64, :] = halves(tails[i : i + 64, :])

    def mul(a, b):
        return lax.dot_general(a, b, (((1,), (1,)), ((), ())), preferred_element_type=F32)

    @pl.loop(0, steps)
    def _(j):
        slot = lax.rem(j, 2)
        fetch(j, slot).wait()

        @pl.when(j + 1 < steps)
        def _():
            fetch(j + 1, 1 - slot).start()

        rh, rl = halves(rbuf[slot])
        acc = mul(high[...], rh) + mul(low[...], rh) + mul(high[...], rl)
        cols = pl.ds(pl.multiple_of(j * SB, SB), SB)
        own[:, cols] = acc[:half]
        oth[:, cols] = acc[half:]


def gradients(softness, layout, pieces, risk):
    n_inst, n_scen = risk.shape
    rows = C * XH * Z * 8
    shape = jax.ShapeDtypeStruct((rows // 2, n_inst + EXT), F32)
    return pl.pallas_call(
        functools.partial(grad_kernel, softness, layout),
        out_shape=[shape, shape],
        in_specs=[VMEM] * len(pieces) + [HBM],
        out_specs=[VMEM] * 2,
        scratch_shapes=[
            pltpu.VMEM((2, SB, n_scen), F32),
            pltpu.VMEM((rows, n_scen), F32),
            pltpu.VMEM((rows, EXT), F32),
            pltpu.VMEM((rows, n_scen), BF16),
            pltpu.VMEM((rows, n_scen), BF16),
            pltpu.SemaphoreType.DMA((2,)),
        ],
        compiler_params=pltpu.CompilerParams(vmem_limit_bytes=24 << 20),
        cost_estimate=pl.CostEstimate(
            flops=6 * rows * n_inst * n_scen, bytes_accessed=8 << 20, transcendentals=rows * n_scen
        ),
    )(*pieces, risk)


def merge(parts):
    peaks = [p[:, -EXT : -EXT + 1] for p in parts]
    peak = peaks[0]
    for other in peaks[1:]:
        peak = jnp.maximum(peak, other)
    total = None
    for part, own_peak in zip(parts, peaks, strict=True):
        term = part * jnp.exp(own_peak - peak)
        total = term if total is None else total + term
    lane = lax.broadcasted_iota(jnp.int32, (total.shape[0], EXT), 1)
    return total[:, :-EXT], jnp.where(lane < 32, peak, total[:, -EXT:])


def merge_owned(blocks):
    above = [pltpu.roll(b, 32, 1) for b in blocks]
    largest, peak = blocks[0], above[0]
    for b, a in zip(blocks[1:], above[1:], strict=True):
        largest, peak = jnp.maximum(largest, b), jnp.maximum(peak, a)
    total = sum(b * jnp.exp(a - peak) for b, a in zip(blocks, above, strict=True))
    lane = lax.broadcasted_iota(jnp.int32, (8, EXT), 1)
    return jnp.where(lane < 96, largest, total)


def put(out, rows, parts, owned=None):
    data, stats = merge(parts)
    out[rows, :-EXT] = data
    if owned is not None:
        lane = lax.broadcasted_iota(jnp.int32, stats.shape, 1)
        stats = jnp.where(lane < 64, stats, owned)
    out[rows, -EXT:] = stats


def call(kernel, outs, *args):
    return pl.pallas_call(
        kernel,
        out_shape=[jax.ShapeDtypeStruct(s, F32) for s in outs],
        in_specs=[VMEM] * len(args),
        out_specs=[VMEM] * len(outs),
        compiler_params=pltpu.CompilerParams(vmem_limit_bytes=4 << 20),
        cost_estimate=pl.CostEstimate(
            flops=sum(a.size for a in args), bytes_accessed=8 * sum(a.size for a in args), transcendentals=0
        ),
    )(*args)


LOW, HIGH = slice(0, 8), slice(8, 16)


def core_kernel(own, came, z4a, z4b, z0, z1, z2, z3, z5, z6, z7, acc):
    owned = merge_owned([own[LOW, -EXT:], came[LOW, -EXT:]])
    acc[...] = owned
    for d, out in enumerate((z0, z1, z2, z3, None, z5, z6, z7)):
        for h in range(2):
            rows = slice(d * 16 + h * 8, d * 16 + h * 8 + 8)
            parts = [own[rows, :], came[rows, :]]
            if d == 4:
                put((z4a, z4b)[h], LOW, parts, owned)
            else:
                put(out, (LOW, HIGH)[h], parts)


def first_kernel(z3, up, z5, down, acc, out3, out5, out_acc):
    put(out3, LOW, [z3[LOW, :], up[...]], up[:, -EXT:])
    out3[HIGH, :] = z3[HIGH, :]
    out5[LOW, :-EXT] = z5[LOW, :-EXT]
    lane = lax.broadcasted_iota(jnp.int32, (8, EXT), 1)
    out5[LOW, -EXT:] = jnp.where(lane < 64, z5[LOW, -EXT:], down[:, -EXT:])
    put(out5, HIGH, [z5[HIGH, :], down[...]])
    out_acc[...] = merge_owned([acc[...], up[:, -EXT:], down[:, -EXT:]])


def next_kernel(a, up, b, down, acc, out_a, out_b, out_acc):
    put(out_a, LOW, [a[LOW, :], up[LOW, :]], up[LOW, -EXT:])
    put(out_a, HIGH, [a[HIGH, :], up[HIGH, :]])
    put(out_b, LOW, [b[LOW, :], down[LOW, :]], down[LOW, -EXT:])
    put(out_b, HIGH, [b[HIGH, :], down[HIGH, :]])
    out_acc[...] = merge_owned([acc[...], up[LOW, -EXT:], down[LOW, -EXT:]])


def last_kernel(a, up, down, acc, out_own, out_oth):
    owned = merge_owned([acc[...], up[LOW, -EXT:]])
    for h, out in ((LOW, out_own), (HIGH, out_oth)):
        put(out, LOW, [a[h, :], up[h, :], down[h, :]], owned)


def end_kernel(scenarios, own0, came0, own1, came1, out, margin):
    for h, parts in ((LOW, (own0, came0)), (HIGH, (own1, came1))):
        data, stats = merge([p[...] for p in parts])
        out[h, :] = -data / stats[:, 32:33]
        owned = merge_owned([p[:, -EXT:] for p in parts])
        margin[h, :] = pltpu.roll(owned, 32, 1) + jnp.log(owned) - math.log(scenarios)


def body(positions, grid, risk):
    accounts, n_inst = positions.shape
    n_scen = risk.shape[1]
    softness = 8.0 * math.sqrt(n_inst * Y * XL)
    scenarios = n_scen * XH * Z * C

    own, oth, b0, b1, b2, b3 = profits(positions, grid, risk)
    x0 = send(oth, "xl", 1)
    r1, r3, r2 = send(b1, "y", 1), send(b3, "y", -1), send(b2, "y", 2)
    near = [own[d * 32 : d * 32 + 32] + x0[d * 32 : d * 32 + 32] for d in range(Y)]
    pair = b0 + r1 + r3 + r2
    q1, q3, q2 = send(near[1], "y", 1), send(near[3], "y", -1), send(near[2], "y", 2)
    x1 = send(pair, "xl", 1)
    m0 = near[0] + q1 + q3 + q2
    both = pair + jnp.concatenate([x1[32:], x1[:32]])

    c3, c1, c2 = send(m0, "y", 1), send(m0, "y", -1), send(m0, "y", 2)
    row = jnp.concatenate([m0, c1, c2, c3])
    rest = send(row, "xl", 1)
    e3, e1, e2 = send(both, "y", 1), send(both, "y", -1), send(both, "y", 2)

    ends = []
    for layout, pieces in (
        ([[(d, 0) for d in range(Y)], [(d, 1) for d in range(Y)]], (row, rest)),
        ([[(d, e) for e in range(XL)] for d in range(Y)], (both, e1, e2, e3)),
    ):
        kept, gone = gradients(softness, layout, pieces, risk)
        came = send(gone, "c", 1)
        width = n_inst + EXT
        *z, acc = call(core_kernel, [(8, width)] * 2 + [(16, width)] * 7 + [(8, EXT)], kept, came)
        z4a, z4b, z0, z1, z2, z3, z5, z6, z7 = z
        shapes = [(16, width)] * 2 + [(8, EXT)]
        up, down = send(z4a, "z", 1), send(z4b, "z", -1)
        up, down, acc = call(first_kernel, shapes, z3, up, z5, down, acc)
        for a, b in ((z2, z6), (z1, z7)):
            up, down = send(up, "z", 1), send(down, "z", -1)
            up, down, acc = call(next_kernel, shapes, a, up, b, down, acc)
        up, down = send(up, "z", 1), send(down, "z", -1)
        keep, go = call(last_kernel, [(8, width)] * 2, z0, up, down, acc)
        ends += [keep, send(go, "xh", 1)]
    last = functools.partial(end_kernel, scenarios)
    gradient, margin = call(last, [(16, n_inst), (16, EXT)], *ends)
    margin = margin[:, 96:100].reshape(2, 8, 4).transpose(2, 0, 1).reshape(64)
    return margin, gradient


def solution(mesh):
    torus = Mesh(mesh.devices.reshape(Y, XL, XH, Z, C), ("y", "xl", "xh", "z", "c"))
    inst, scen = ("y", "xl"), ("xh", "z", "c")
    return jax.shard_map(
        body,
        mesh=torus,
        in_specs=(P(None, inst), P(None, inst), P(inst, scen)),
        out_specs=(P(inst), P(scen, inst)),
        check_vma=False,
    )
```

```python
import functools
import math

import jax
import jax.numpy as jnp
from jax import lax
from jax.experimental import pallas as pl
from jax.experimental.pallas import tpu as pltpu
from jax.sharding import Mesh
from jax.sharding import PartitionSpec as P

Y, XL, XH, Z, C = 4, 2, 2, 8, 2
F32, BF16 = jnp.float32, jnp.bfloat16
VMEM = pl.BlockSpec(memory_space=pltpu.VMEM)
HBM = pl.BlockSpec(memory_space=pltpu.HBM)
SB, KB = 256, 256
EXT = 128


def send(x, axis, shift):
    n = lax.axis_size(axis)
    return lax.ppermute(x, axis, [(i, (i + shift) % n) for i in range(n)])


def halves(x):
    high = x.astype(BF16)
    return high, (x - high.astype(F32)).astype(BF16)


def first_pnl_kernel(
    pos, grid_in, risk, oth, b1, b2, b3, high, low, rest, posbuf, grid, rbuf, held, psem, gsem, rsem
):
    y, xl = lax.axis_index("y"), lax.axis_index("xl")
    n_inst, n_scen = risk.shape
    steps = n_inst // KB
    grid_copy = pltpu.make_async_copy(grid_in, grid, gsem)

    def fetch(q):
        part = pl.ds(pl.multiple_of(q * KB, KB), KB)
        return (
            pltpu.make_async_copy(pos.at[:, part], posbuf.at[q], psem.at[q]),
            pltpu.make_async_copy(risk.at[part, :], rbuf.at[q], rsem.at[q]),
        )

    grid_copy.start()
    for q in range(steps):
        for copy in fetch(q):
            copy.start()
    grid_copy.wait()

    blocks = [(held, 0, d, 1) for d in range(Y)]
    blocks += [(held, 1, d, e) for d in range(1, Y) for e in range(XL)]
    blocks += [(rest, 0, d, 0) for d in range(Y)] + [(rest, 1, 0, e) for e in range(XL)]
    outs = ((0, oth), (128, b1), (192, b2), (256, b3))

    def step(q, first):
        for copy in fetch(q):
            copy.wait()
        base = pl.multiple_of(q * KB, KB)
        part, at = pl.ds(base, KB), 0
        for out, k, d, e in blocks:
            if (k, d, e) == (0, 0, 0):
                at = 0
            o = lax.rem(y + d, Y) * 2 + lax.rem(xl + e, XL)
            live = [grid[o, q * (KB // 128) + i].astype(F32) for i in range(KB // 128)]
            for pair in range(2):
                row = pl.multiple_of(o * 64 + pair * 32 + k * 8, 8)
                for i in range(KB // 128):
                    lanes = slice(i * 128, i * 128 + 128)
                    x = [posbuf[q, pl.ds(row + 16 * h, 8), lanes] for h in range(2)]
                    x = jnp.concatenate(x, axis=0).astype(F32) * live[i]
                    if out is held:
                        out[at : at + 16, lanes] = x.astype(BF16)
                    else:
                        out[at : at + 16, pl.ds(pl.multiple_of(base + i * 128, 128), 128)] = x.astype(BF16)
                at += 16
        for i in range(0, KB, 128):
            rows = pl.ds(pl.multiple_of(base + i, 128), 128)
            high[rows, :], low[rows, :] = halves(rbuf[q, i : i + 128, :])
        for i in range(0, n_scen, SB):
            cols = slice(i, i + SB)
            acc = jnp.dot(held[...], high[part, cols], preferred_element_type=F32)
            acc += jnp.dot(held[...], low[part, cols], preferred_element_type=F32)
            for begin, out in outs:
                term = acc[begin : begin + out.shape[0]]
                out[:, cols] = term if first else out[:, cols] + term

    step(0, True)
    pl.loop(1, steps)(functools.partial(step, first=False))


def first_profits(positions, grid, risk):
    rows, n = risk.shape
    accounts = positions.shape[0]
    outs = [((r, n), F32) for r in (128, 64, 64, 64)] + [((rows, n), BF16)] * 2 + [((192, rows), BF16)]
    return pl.pallas_call(
        first_pnl_kernel,
        out_shape=[jax.ShapeDtypeStruct(*o) for o in outs],
        in_specs=[HBM] * 3,
        out_specs=[VMEM] * len(outs),
        scratch_shapes=[
            pltpu.VMEM((rows // KB, accounts, KB), jnp.int32),
            pltpu.SMEM(grid.shape, jnp.int32),
            pltpu.VMEM((rows // KB, KB, n), F32),
            pltpu.VMEM((320, KB), BF16),
            pltpu.SemaphoreType.DMA((rows // KB,)),
            pltpu.SemaphoreType.DMA,
            pltpu.SemaphoreType.DMA((rows // KB,)),
        ],
        compiler_params=pltpu.CompilerParams(vmem_limit_bytes=24 << 20),
        cost_estimate=pl.CostEstimate(flops=4 * 320 * rows * n, bytes_accessed=12 << 20, transcendentals=0),
    )(*(pltpu.with_memory_space_constraint(a, pltpu.HBM) for a in (positions, grid, risk)))


def rest_pnl_kernel(rest, high, low, own, b0):
    @pl.loop(0, high.shape[1] // SB)
    def _(j):
        cols = pl.ds(pl.multiple_of(j * SB, SB), SB)
        acc = jnp.dot(rest[...], high[:, cols], preferred_element_type=F32)
        acc += jnp.dot(rest[...], low[:, cols], preferred_element_type=F32)
        own[:, cols] = acc[:128]
        b0[:, cols] = acc[128:]


def rest_profits(rest, high, low):
    n = high.shape[1]
    return pl.pallas_call(
        rest_pnl_kernel,
        out_shape=[jax.ShapeDtypeStruct((r, n), F32) for r in (128, 64)],
        in_specs=[VMEM] * 3,
        out_specs=[VMEM] * 2,
        compiler_params=pltpu.CompilerParams(vmem_limit_bytes=6 << 20),
        cost_estimate=pl.CostEstimate(flops=4 * rest.size * n, bytes_accessed=12 << 20, transcendentals=0),
    )(rest, high, low)


def tails_of(softness, pieces, layout, both, put_stats):
    lane = lax.broadcasted_iota(jnp.int32, (8, EXT), 1)
    owned, at, rows = jnp.zeros((8, EXT), F32), 0, both.shape[0] // 2
    for ref, blocks in zip(pieces, layout, strict=True):
        for b, (d, e) in enumerate(blocks):
            score = ref[b * 32 : b * 32 + 32, :] * (-1.0 / softness)
            peak = jnp.max(score, axis=1, keepdims=True)
            tail = jnp.exp(score - peak)
            total = jnp.sum(tail, axis=1, keepdims=True)
            both[at : at + 32, :], both[rows + at : rows + at + 32, :] = halves(tail)
            for t in range(4):
                part = slice(t * 8, t * 8 + 8)
                put_stats(at + t * 8, jnp.where(lane < 32, peak[part], jnp.where(lane < 64, total[part], 0.0)))
                if (d, e) == (0, 0):
                    owned = jnp.where(lane == 64 + t, peak[part], owned)
                    owned = jnp.where(lane == 96 + t, total[part], owned)
            at += 32
    return owned


def block_product(both, high, low, i):
    rows = both.shape[0] // 2

    def mul(a, b):
        return lax.dot_general(a, b, (((1,), (1,)), ((), ())), preferred_element_type=F32)

    part = pl.ds(pl.multiple_of(i * SB, SB), SB)
    twice = mul(both[...], high[part, :])
    return twice[:rows] + twice[rows:] + mul(both[:rows, :], low[part, :])


def early_kernel(softness, layout, *refs):
    pieces, (high, low, out, both) = refs[: len(layout)], refs[len(layout) :]
    n_inst = high.shape[0]

    def put_stats(row, stats):
        out[row : row + 8, n_inst:] = stats

    owned = tails_of(softness, pieces, layout, both, put_stats)
    lane = lax.broadcasted_iota(jnp.int32, (8, EXT), 1)
    out[:8, n_inst:] = jnp.where(lane < 64, out[:8, n_inst:], owned)

    @pl.loop(0, n_inst // SB)
    def _(i):
        out[:, pl.ds(pl.multiple_of(i * SB, SB), SB)] = block_product(both, high, low, i)


def late_kernel(softness, layout, done_layout, *refs):
    pieces, (done, high, low, own, oth, both, full) = refs[: len(layout)], refs[len(layout) :]
    y, xl, xh, z, c = (lax.axis_index(a) for a in ("y", "xl", "xh", "z", "c"))
    n_inst = high.shape[0]
    lane = lax.broadcasted_iota(jnp.int32, (8, EXT), 1)

    def places(blocks):
        found = []
        for d, e in blocks:
            o = lax.rem(y + d, Y) * 2 + lax.rem(xl + e, XL)
            other_xh = jnp.where(o // 4 == xh, 0, 1)
            for t in range(4):
                dz = lax.rem(lax.rem(o, 4) * 2 + t // 2 + Z - z, Z)
                dc = jnp.where(c == t % 2, 0, 1)
                found.append(pl.ds(pl.multiple_of(((dc * Z + dz) * XH + other_xh) * 8, 8), 8))
        return found

    place = places(sum(layout, []))

    def put_stats(row, stats):
        full[place[row // 8], n_inst:] = stats

    tails_of(softness, pieces, layout, both, put_stats)
    for g, rows in enumerate(places(done_layout)):
        part = slice(g * 8, g * 8 + 8)
        full[rows, :n_inst] = done[part, :n_inst]
        full[rows, n_inst:] = jnp.where(lane < 64, done[part, n_inst:], 0.0)

    @pl.loop(0, n_inst // SB)
    def _(i):
        acc = block_product(both, high, low, i)
        cols = pl.ds(pl.multiple_of(i * SB, SB), SB)
        for g, rows in enumerate(place):
            full[rows, cols] = acc[g * 8 : g * 8 + 8]

    half = full.shape[0] // 2
    for out, first in ((own, 0), (oth, half)):
        for row in range(0, half, 8):
            out[row : row + 8, :] = full[first + row : first + row + 8, :]
        out[:8, n_inst:] = jnp.where(lane < 64, full[first : first + 8, n_inst:], done[:8, n_inst:])


def gradients(kernel, pieces, high, low, out_rows, scratch, done=()):
    n_inst, n_scen = high.shape
    rows = sum(p.shape[0] for p in pieces)
    return pl.pallas_call(
        kernel,
        out_shape=[jax.ShapeDtypeStruct((r, n_inst + EXT), F32) for r in out_rows],
        in_specs=[VMEM] * (len(pieces) + len(done) + 2),
        out_specs=[VMEM] * len(out_rows),
        scratch_shapes=[pltpu.VMEM((2 * rows, n_scen), BF16)] + scratch,
        compiler_params=pltpu.CompilerParams(vmem_limit_bytes=12 << 20),
        cost_estimate=pl.CostEstimate(
            flops=6 * rows * n_inst * n_scen, bytes_accessed=8 << 20, transcendentals=rows * n_scen
        ),
    )(*pieces, *done, high, low)


def merge(parts):
    peaks = [p[:, -EXT : -EXT + 1] for p in parts]
    peak = peaks[0]
    for other in peaks[1:]:
        peak = jnp.maximum(peak, other)
    total = None
    for part, own_peak in zip(parts, peaks, strict=True):
        term = part * jnp.exp(own_peak - peak)
        total = term if total is None else total + term
    lane = lax.broadcasted_iota(jnp.int32, (total.shape[0], EXT), 1)
    return total[:, :-EXT], jnp.where(lane < 32, peak, total[:, -EXT:])


def merge_owned(blocks):
    above = [pltpu.roll(b, 32, 1) for b in blocks]
    largest, peak = blocks[0], above[0]
    for b, a in zip(blocks[1:], above[1:], strict=True):
        largest, peak = jnp.maximum(largest, b), jnp.maximum(peak, a)
    total = sum(b * jnp.exp(a - peak) for b, a in zip(blocks, above, strict=True))
    lane = lax.broadcasted_iota(jnp.int32, (8, EXT), 1)
    return jnp.where(lane < 96, largest, total)


def put(out, rows, parts, owned=None):
    data, stats = merge(parts)
    out[rows, :-EXT] = data
    if owned is not None:
        lane = lax.broadcasted_iota(jnp.int32, stats.shape, 1)
        stats = jnp.where(lane < 64, stats, owned)
    out[rows, -EXT:] = stats


def call(kernel, outs, *args):
    return pl.pallas_call(
        kernel,
        out_shape=[jax.ShapeDtypeStruct(s, F32) for s in outs],
        in_specs=[VMEM] * len(args),
        out_specs=[VMEM] * len(outs),
        compiler_params=pltpu.CompilerParams(vmem_limit_bytes=4 << 20),
        cost_estimate=pl.CostEstimate(
            flops=sum(a.size for a in args), bytes_accessed=8 * sum(a.size for a in args), transcendentals=0
        ),
    )(*args)


LOW, HIGH = slice(0, 8), slice(8, 16)


def put_rows(out, *parts, owned=None):
    for rows in (LOW, HIGH):
        put(out, rows, [p[rows, :] for p in parts], owned if rows == LOW else None)


def core_kernel(own, came, *outs):
    owned = merge_owned([own[LOW, -EXT:], came[LOW, -EXT:]])
    outs[-1][...] = owned
    for d, out in enumerate(outs[:-1]):
        rows = slice(d * 16, d * 16 + 16)
        put_rows(out, own.at[rows, :], came.at[rows, :], owned=owned if d in (3, 4, 5) else None)


def next_kernel(own, came, *refs):
    out, acc = refs[-2:]
    owned = came[LOW, -EXT:]
    put_rows(out, own, came, owned=owned)
    acc[...] = merge_owned([refs[0][...], owned]) if len(refs) == 3 else owned


def last_kernel(*refs):
    kept, gone = refs[-2:]
    for group, rows in zip((refs[:5], refs[5:10]), (LOW, HIGH), strict=True):
        here, flows, accs = group[0], group[1:3], group[3:]
        owned = merge_owned([a[...] for a in accs] + [f[LOW, -EXT:] for f in flows])
        for h, out in ((LOW, kept), (HIGH, gone)):
            put(out, rows, [here[h, :]] + [f[h, :] for f in flows], owned)


def end_kernel(scenarios, kept, came, out, margin):
    values = []
    for rows in (LOW, HIGH):
        data, stats = merge([kept[rows, :], came[rows, :]])
        out[rows, :] = -data / stats[:, 32:33]
        owned = merge_owned([kept[rows, -EXT:], came[rows, -EXT:]])
        values.append(pltpu.roll(owned, 32, 1) + jnp.log(owned) - math.log(scenarios))
    values.append(jnp.zeros((EXT - 16, EXT), F32))
    columns = jnp.concatenate(values, axis=0).T[96:104, :]
    line = columns[:1]
    for t in range(1, 4):
        line += pltpu.roll(columns, 16 * t, 1)[t : t + 1]
    margin[...] = line[:, :64]


def body(positions, grid, risk):
    _, n_inst = positions.shape
    n_scen = risk.shape[1]
    softness = 8.0 * math.sqrt(n_inst * Y * XL)
    scenarios = n_scen * XH * Z * C

    oth, b1, b2, b3, high, low, remaining = first_profits(positions, grid, risk)
    x0 = send(oth, "xl", 1)
    r1, r3, r2 = send(b1, "y", 1), send(b3, "y", -1), send(b2, "y", 2)
    own, b0 = rest_profits(remaining, high, low)
    near = [own[d * 32 : d * 32 + 32] + x0[d * 32 : d * 32 + 32] for d in range(Y)]
    pair = b0 + r1 + r3 + r2
    q1, q3, q2 = (send(near[d], "y", s) for d, s in ((1, 1), (3, -1), (2, 2)))
    x1 = send(pair, "xl", 1)
    m0 = near[0] + q1 + q3 + q2
    both = pair + jnp.concatenate([x1[32:], x1[:32]])

    c3, c1, c2 = (send(m0, "y", s) for s in (1, -1, 2))
    row = jnp.concatenate([m0, c1, c2, c3])
    rest = send(row, "xl", 1)
    e3, e1, e2 = (send(both, "y", s) for s in (1, -1, 2))

    width = n_inst + EXT
    groups = (
        ((row,), [[(d, 0) for d in range(Y)]], (rest,), [[(d, 1) for d in range(Y)]]),
        ((both,), [[(0, 0), (0, 1)]], (e1, e2, e3), [[(d, 0), (d, 1)] for d in (1, 2, 3)]),
    )
    dones = []
    for pieces, layout, _, _ in groups:
        kernel = functools.partial(early_kernel, softness, layout)
        dones += gradients(kernel, pieces, high, low, [pieces[0].shape[0]], [])
    dones = lax.optimization_barrier(tuple(dones))

    ends = []
    for (_, layout, late_pieces, late_layout), done in zip(groups, dones, strict=True):
        kernel = functools.partial(late_kernel, softness, late_layout, layout[0])
        scratch = [pltpu.VMEM((256, width), F32)]
        kept, gone = gradients(kernel, late_pieces, high, low, [128, 128], scratch, [done])
        came = send(gone, "c", 1)
        *at, acc = call(core_kernel, [(16, width)] * Z + [(8, EXT)], kept, came)
        up, down = ((4, 3, 2, 1), (5, 6, 7)) if not ends else ((3, 2, 1), (4, 5, 6, 7))
        flows, accs = [], []
        for hops, shift in ((up, 1), (down, -1)):
            kind = [acc] if len(hops) == 4 else []
            flow = send(at[hops[0]], "z", shift)
            for d in hops[1:]:
                flow, *kind = call(next_kernel, [(16, width), (8, EXT)], at[d], flow, *kind)
                flow = send(flow, "z", shift)
            flows.append(flow)
            accs += kind
        ends += [at[0], *flows, *accs]
    kept, gone = call(last_kernel, [(16, width)] * 2, *ends)
    last = functools.partial(end_kernel, scenarios)
    gradient, margin = call(last, [(16, n_inst), (1, 64)], kept, send(gone, "xh", 1))
    margin = margin.reshape(64)
    return margin, gradient


def solution(mesh):
    torus = Mesh(mesh.devices.reshape(Y, XL, XH, Z, C), ("y", "xl", "xh", "z", "c"))
    inst, scen = ("y", "xl"), ("xh", "z", "c")
    return jax.shard_map(
        body,
        mesh=torus,
        in_specs=(P(None, inst), P(None, inst), P(inst, scen)),
        out_specs=(P(inst), P(scen, inst)),
        check_vma=False,
    )
```

```python
import functools
import math

import jax
import jax.numpy as jnp
from jax import lax
from jax.experimental import pallas as pl
from jax.experimental.pallas import tpu as pltpu
from jax.sharding import Mesh
from jax.sharding import PartitionSpec as P

Y, XL, XH, Z, C = 4, 2, 2, 8, 2
F32, BF16 = jnp.float32, jnp.bfloat16
VMEM = pl.BlockSpec(memory_space=pltpu.VMEM)
HBM = pl.BlockSpec(memory_space=pltpu.HBM)
SB, KB = 256, 256
EXT = 128


def send(x, axis, shift):
    n = lax.axis_size(axis)
    return lax.ppermute(x, axis, [(i, (i + shift) % n) for i in range(n)])


def halves(x):
    high = x.astype(BF16)
    return high, (x - high.astype(F32)).astype(BF16)


def first_pnl_kernel(
    pos, grid_in, risk, oth, b1, b2, b3, high, low, rest, posbuf, grid, rbuf, held, psem, gsem, rsem
):
    y, xl = lax.axis_index("y"), lax.axis_index("xl")
    n_inst, n_scen = risk.shape
    steps = n_inst // KB
    grid_copy = pltpu.make_async_copy(grid_in, grid, gsem)

    def fetch(q):
        part = pl.ds(pl.multiple_of(q * KB, KB), KB)
        return (
            pltpu.make_async_copy(pos.at[:, part], posbuf.at[q], psem.at[q]),
            pltpu.make_async_copy(risk.at[part, :], rbuf.at[q], rsem.at[q]),
        )

    grid_copy.start()
    for q in range(steps):
        for copy in fetch(q):
            copy.start()
    grid_copy.wait()

    blocks = [(held, 0, d, 1) for d in range(Y)]
    blocks += [(held, 1, d, e) for d in range(1, Y) for e in range(XL)]
    blocks += [(rest, 0, d, 0) for d in range(Y)] + [(rest, 1, 0, e) for e in range(XL)]
    outs = ((0, oth), (128, b1), (192, b2), (256, b3))

    def step(q, first):
        for copy in fetch(q):
            copy.wait()
        base = pl.multiple_of(q * KB, KB)
        part, at = pl.ds(base, KB), 0
        for out, k, d, e in blocks:
            if (k, d, e) == (0, 0, 0):
                at = 0
            o = lax.rem(y + d, Y) * 2 + lax.rem(xl + e, XL)
            live = [grid[o, q * (KB // 128) + i].astype(F32) for i in range(KB // 128)]
            for pair in range(2):
                row = pl.multiple_of(o * 64 + pair * 32 + k * 8, 8)
                for i in range(KB // 128):
                    lanes = slice(i * 128, i * 128 + 128)
                    x = [posbuf[q, pl.ds(row + 16 * h, 8), lanes] for h in range(2)]
                    x = jnp.concatenate(x, axis=0).astype(F32) * live[i]
                    if out is held:
                        out[at : at + 16, lanes] = x.astype(BF16)
                    else:
                        out[at : at + 16, pl.ds(pl.multiple_of(base + i * 128, 128), 128)] = x.astype(BF16)
                at += 16
        for i in range(0, KB, 128):
            rows = pl.ds(pl.multiple_of(base + i, 128), 128)
            high[rows, :], low[rows, :] = halves(rbuf[q, i : i + 128, :])
        for i in range(0, n_scen, SB):
            cols = slice(i, i + SB)
            acc = jnp.dot(held[...], high[part, cols], preferred_element_type=F32)
            acc += jnp.dot(held[...], low[part, cols], preferred_element_type=F32)
            for begin, out in outs:
                term = acc[begin : begin + out.shape[0]]
                out[:, cols] = term if first else out[:, cols] + term

    step(0, True)
    pl.loop(1, steps)(functools.partial(step, first=False))


def first_profits(positions, grid, risk):
    rows, n = risk.shape
    accounts = positions.shape[0]
    outs = [((r, n), F32) for r in (128, 64, 64, 64)] + [((rows, n), BF16)] * 2 + [((192, rows), BF16)]
    return pl.pallas_call(
        first_pnl_kernel,
        out_shape=[jax.ShapeDtypeStruct(*o) for o in outs],
        in_specs=[HBM] * 3,
        out_specs=[VMEM] * len(outs),
        scratch_shapes=[
            pltpu.VMEM((rows // KB, accounts, KB), jnp.int32),
            pltpu.SMEM(grid.shape, jnp.int32),
            pltpu.VMEM((rows // KB, KB, n), F32),
            pltpu.VMEM((320, KB), BF16),
            pltpu.SemaphoreType.DMA((rows // KB,)),
            pltpu.SemaphoreType.DMA,
            pltpu.SemaphoreType.DMA((rows // KB,)),
        ],
        compiler_params=pltpu.CompilerParams(vmem_limit_bytes=24 << 20),
        cost_estimate=pl.CostEstimate(flops=4 * 320 * rows * n, bytes_accessed=12 << 20, transcendentals=0),
    )(*(pltpu.with_memory_space_constraint(a, pltpu.HBM) for a in (positions, grid, risk)))


def rest_pnl_kernel(rest, high, low, own, b0):
    @pl.loop(0, high.shape[1] // SB)
    def _(j):
        cols = pl.ds(pl.multiple_of(j * SB, SB), SB)
        acc = jnp.dot(rest[...], high[:, cols], preferred_element_type=F32)
        acc += jnp.dot(rest[...], low[:, cols], preferred_element_type=F32)
        own[:, cols] = acc[:128]
        b0[:, cols] = acc[128:]


def rest_profits(rest, high, low):
    n = high.shape[1]
    return pl.pallas_call(
        rest_pnl_kernel,
        out_shape=[jax.ShapeDtypeStruct((r, n), F32) for r in (128, 64)],
        in_specs=[VMEM] * 3,
        out_specs=[VMEM] * 2,
        compiler_params=pltpu.CompilerParams(vmem_limit_bytes=6 << 20),
        cost_estimate=pl.CostEstimate(flops=4 * rest.size * n, bytes_accessed=12 << 20, transcendentals=0),
    )(rest, high, low)


def tails_of(softness, pieces, layout, both, put_stats, at=0):
    lane = lax.broadcasted_iota(jnp.int32, (8, EXT), 1)
    owned, rows = jnp.zeros((8, EXT), F32), both.shape[0] // 2
    for ref, blocks in zip(pieces, layout, strict=True):
        for b, (d, e) in enumerate(blocks):
            score = ref[b * 32 : b * 32 + 32, :] * (-1.0 / softness)
            peak = jnp.max(score, axis=1, keepdims=True)
            tail = jnp.exp(score - peak)
            total = jnp.sum(tail, axis=1, keepdims=True)
            both[at : at + 32, :], both[rows + at : rows + at + 32, :] = halves(tail)
            for t in range(4):
                part = slice(t * 8, t * 8 + 8)
                put_stats(at + t * 8, jnp.where(lane < 32, peak[part], jnp.where(lane < 64, total[part], 0.0)))
                if (d, e) == (0, 0):
                    owned = jnp.where(lane == 64 + t, peak[part], owned)
                    owned = jnp.where(lane == 96 + t, total[part], owned)
            at += 32
    return owned


def block_product(both, high, low, i):
    rows = both.shape[0] // 2

    def mul(a, b):
        return lax.dot_general(a, b, (((1,), (1,)), ((), ())), preferred_element_type=F32)

    part = pl.ds(pl.multiple_of(i * SB, SB), SB)
    twice = mul(both[...], high[part, :])
    return twice[:rows] + twice[rows:] + mul(both[:rows, :], low[part, :])


def early_kernel(softness, layouts, *refs):
    n = len(layouts)
    pieces, (high, low), outs, both = refs[:n], refs[n : n + 2], refs[n + 2 : -1], refs[-1]
    n_inst, at, starts = high.shape[0], 0, []
    lane = lax.broadcasted_iota(jnp.int32, (8, EXT), 1)
    for piece, layout, out in zip(pieces, layouts, outs, strict=True):

        def put_stats(row, stats, out=out, at=at):
            out[row - at : row - at + 8, n_inst:] = stats

        owned = tails_of(softness, [piece], [layout], both, put_stats, at)
        out[:8, n_inst:] = jnp.where(lane < 64, out[:8, n_inst:], owned)
        starts.append(at)
        at += piece.shape[0]

    @pl.loop(0, n_inst // SB)
    def _(i):
        acc = block_product(both, high, low, i)
        cols = pl.ds(pl.multiple_of(i * SB, SB), SB)
        for first, out in zip(starts, outs, strict=True):
            out[:, cols] = acc[first : first + out.shape[0]]


def late_kernel(softness, layout, done_layout, *refs):
    pieces, (done, high, low, own, oth, both, full) = refs[: len(layout)], refs[len(layout) :]
    y, xl, xh, z, c = (lax.axis_index(a) for a in ("y", "xl", "xh", "z", "c"))
    n_inst = high.shape[0]
    lane = lax.broadcasted_iota(jnp.int32, (8, EXT), 1)

    def places(blocks):
        found = []
        for d, e in blocks:
            o = lax.rem(y + d, Y) * 2 + lax.rem(xl + e, XL)
            other_xh = jnp.where(o // 4 == xh, 0, 1)
            for t in range(4):
                dz = lax.rem(lax.rem(o, 4) * 2 + t // 2 + Z - z, Z)
                dc = jnp.where(c == t % 2, 0, 1)
                found.append(pl.ds(pl.multiple_of(((dc * Z + dz) * XH + other_xh) * 8, 8), 8))
        return found

    place = places(sum(layout, []))

    def put_stats(row, stats):
        full[place[row // 8], n_inst:] = stats

    tails_of(softness, pieces, layout, both, put_stats)
    for g, rows in enumerate(places(done_layout)):
        part = slice(g * 8, g * 8 + 8)
        full[rows, :n_inst] = done[part, :n_inst]
        full[rows, n_inst:] = jnp.where(lane < 64, done[part, n_inst:], 0.0)

    @pl.loop(0, n_inst // SB)
    def _(i):
        acc = block_product(both, high, low, i)
        cols = pl.ds(pl.multiple_of(i * SB, SB), SB)
        for g, rows in enumerate(place):
            full[rows, cols] = acc[g * 8 : g * 8 + 8]

    half = full.shape[0] // 2
    for out, first in ((own, 0), (oth, half)):
        for row in range(0, half, 8):
            out[row : row + 8, :] = full[first + row : first + row + 8, :]
        out[:8, n_inst:] = jnp.where(lane < 64, full[first : first + 8, n_inst:], done[:8, n_inst:])


def gradients(kernel, pieces, high, low, out_rows, scratch, done=()):
    n_inst, n_scen = high.shape
    rows = sum(p.shape[0] for p in pieces)
    return pl.pallas_call(
        kernel,
        out_shape=[jax.ShapeDtypeStruct((r, n_inst + EXT), F32) for r in out_rows],
        in_specs=[VMEM] * (len(pieces) + len(done) + 2),
        out_specs=[VMEM] * len(out_rows),
        scratch_shapes=[pltpu.VMEM((2 * rows, n_scen), BF16)] + scratch,
        compiler_params=pltpu.CompilerParams(vmem_limit_bytes=12 << 20),
        cost_estimate=pl.CostEstimate(
            flops=6 * rows * n_inst * n_scen, bytes_accessed=8 << 20, transcendentals=rows * n_scen
        ),
    )(*pieces, *done, high, low)


def merge(parts):
    peaks = [p[:, -EXT : -EXT + 1] for p in parts]
    peak = peaks[0]
    for other in peaks[1:]:
        peak = jnp.maximum(peak, other)
    total = None
    for part, own_peak in zip(parts, peaks, strict=True):
        term = part * jnp.exp(own_peak - peak)
        total = term if total is None else total + term
    lane = lax.broadcasted_iota(jnp.int32, (total.shape[0], EXT), 1)
    return total[:, :-EXT], jnp.where(lane < 32, peak, total[:, -EXT:])


def merge_owned(blocks):
    above = [pltpu.roll(b, 32, 1) for b in blocks]
    largest, peak = blocks[0], above[0]
    for b, a in zip(blocks[1:], above[1:], strict=True):
        largest, peak = jnp.maximum(largest, b), jnp.maximum(peak, a)
    total = sum(b * jnp.exp(a - peak) for b, a in zip(blocks, above, strict=True))
    lane = lax.broadcasted_iota(jnp.int32, (8, EXT), 1)
    return jnp.where(lane < 96, largest, total)


def put(out, rows, parts, owned=None):
    data, stats = merge(parts)
    out[rows, :-EXT] = data
    if owned is not None:
        lane = lax.broadcasted_iota(jnp.int32, stats.shape, 1)
        stats = jnp.where(lane < 64, stats, owned)
    out[rows, -EXT:] = stats


def call(kernel, outs, *args):
    return pl.pallas_call(
        kernel,
        out_shape=[jax.ShapeDtypeStruct(s, F32) for s in outs],
        in_specs=[VMEM] * len(args),
        out_specs=[VMEM] * len(outs),
        compiler_params=pltpu.CompilerParams(vmem_limit_bytes=4 << 20),
        cost_estimate=pl.CostEstimate(
            flops=sum(a.size for a in args), bytes_accessed=8 * sum(a.size for a in args), transcendentals=0
        ),
    )(*args)


LOW, HIGH = slice(0, 8), slice(8, 16)


def put_rows(out, *parts, owned=None):
    for rows in (LOW, HIGH):
        put(out, rows, [p[rows, :] for p in parts], owned if rows == LOW else None)


def core_kernel(own, came, *outs):
    owned = merge_owned([own[LOW, -EXT:], came[LOW, -EXT:]])
    outs[-1][...] = owned
    for d, out in enumerate(outs[:-1]):
        rows = slice(d * 16, d * 16 + 16)
        put_rows(out, own.at[rows, :], came.at[rows, :], owned=owned if d in (3, 4, 5) else None)


def next_kernel(own, came, *refs):
    out, acc = refs[-2:]
    owned = came[LOW, -EXT:]
    put_rows(out, own, came, owned=owned)
    acc[...] = merge_owned([refs[0][...], owned]) if len(refs) == 3 else owned


def last_kernel(*refs):
    kept, gone = refs[-2:]
    for group, rows in zip((refs[:5], refs[5:10]), (LOW, HIGH), strict=True):
        here, flows, accs = group[0], group[1:3], group[3:]
        owned = merge_owned([a[...] for a in accs] + [f[LOW, -EXT:] for f in flows])
        for h, out in ((LOW, kept), (HIGH, gone)):
            put(out, rows, [here[h, :]] + [f[h, :] for f in flows], owned)


def end_kernel(scenarios, kept, came, out, margin):
    values = []
    for rows in (LOW, HIGH):
        data, stats = merge([kept[rows, :], came[rows, :]])
        out[rows, :] = -data / stats[:, 32:33]
        owned = merge_owned([kept[rows, -EXT:], came[rows, -EXT:]])
        values.append(pltpu.roll(owned, 32, 1) + jnp.log(owned) - math.log(scenarios))
    values.append(jnp.zeros((EXT - 16, EXT), F32))
    columns = jnp.concatenate(values, axis=0).T[96:104, :]
    line = columns[:1]
    for t in range(1, 4):
        line += pltpu.roll(columns, 16 * t, 1)[t : t + 1]
    margin[...] = line[:, :64]


def body(positions, grid, risk):
    _, n_inst = positions.shape
    n_scen = risk.shape[1]
    softness = 8.0 * math.sqrt(n_inst * Y * XL)
    scenarios = n_scen * XH * Z * C

    oth, b1, b2, b3, high, low, remaining = first_profits(positions, grid, risk)
    x0 = send(oth, "xl", 1)
    r1, r3, r2 = send(b1, "y", 1), send(b3, "y", -1), send(b2, "y", 2)
    own, b0 = rest_profits(remaining, high, low)
    near = [own[d * 32 : d * 32 + 32] + x0[d * 32 : d * 32 + 32] for d in range(Y)]
    pair = b0 + r1 + r3 + r2
    q1, q3, q2 = (send(near[d], "y", s) for d, s in ((1, 1), (3, -1), (2, 2)))
    x1 = send(pair, "xl", 1)
    m0 = near[0] + q1 + q3 + q2
    both = pair + jnp.concatenate([x1[32:], x1[:32]])

    c3, c1, c2 = (send(m0, "y", s) for s in (1, -1, 2))
    row = jnp.concatenate([m0, c1, c2, c3])
    rest = send(row, "xl", 1)
    e3, e1, e2 = (send(both, "y", s) for s in (1, -1, 2))

    width = n_inst + EXT
    groups = (
        ((row,), [[(d, 0) for d in range(Y)]], (rest,), [[(d, 1) for d in range(Y)]]),
        ((both,), [[(0, 0), (0, 1)]], (e1, e2, e3), [[(d, 0), (d, 1)] for d in (1, 2, 3)]),
    )
    kernel = functools.partial(early_kernel, softness, [layout[0] for _, layout, _, _ in groups])
    early = [pieces[0] for pieces, _, _, _ in groups]
    dones = gradients(kernel, early, high, low, [p.shape[0] for p in early], [])
    dones = lax.optimization_barrier(tuple(dones))

    ends = []
    for (_, layout, late_pieces, late_layout), done in zip(groups, dones, strict=True):
        kernel = functools.partial(late_kernel, softness, late_layout, layout[0])
        scratch = [pltpu.VMEM((256, width), F32)]
        kept, gone = gradients(kernel, late_pieces, high, low, [128, 128], scratch, [done])
        came = send(gone, "c", 1)
        *at, acc = call(core_kernel, [(16, width)] * Z + [(8, EXT)], kept, came)
        up, down = ((4, 3, 2, 1), (5, 6, 7)) if not ends else ((3, 2, 1), (4, 5, 6, 7))
        flows, accs = [], []
        for hops, shift in ((up, 1), (down, -1)):
            kind = [acc] if len(hops) == 4 else []
            flow = send(at[hops[0]], "z", shift)
            for d in hops[1:]:
                flow, *kind = call(next_kernel, [(16, width), (8, EXT)], at[d], flow, *kind)
                flow = send(flow, "z", shift)
            flows.append(flow)
            accs += kind
        ends += [at[0], *flows, *accs]
    kept, gone = call(last_kernel, [(16, width)] * 2, *ends)
    last = functools.partial(end_kernel, scenarios)
    gradient, margin = call(last, [(16, n_inst), (1, 64)], kept, send(gone, "xh", 1))
    margin = margin.reshape(64)
    return margin, gradient


def solution(mesh):
    torus = Mesh(mesh.devices.reshape(Y, XL, XH, Z, C), ("y", "xl", "xh", "z", "c"))
    inst, scen = ("y", "xl"), ("xh", "z", "c")
    return jax.shard_map(
        body,
        mesh=torus,
        in_specs=(P(None, inst), P(None, inst), P(inst, scen)),
        out_specs=(P(inst), P(scen, inst)),
        check_vma=False,
    )
```
